32 devices in a mesh: row: 4 (over z), col: 4 (over y, x), depth: 2 (over core).
Axes of the slice: x: 2, y: 2, z: 4, core: 2. Of those that a mesh axis runs over, the one named last changes fastest.
Arguments:
- tiles: float32 [4, 4, 96, 256, 256], P('row', 'col', 'depth'), as said below
- tile_rows: int32 [4, 4, 96], P('row', 'col', 'depth'), may hold values from 0 to 127, as said below
- tile_cols: int32 [4, 4, 96], P('row', 'col', 'depth'), may hold values from 0 to 127
- tile_count: int32 [4, 4, 2], P('row', 'col', 'depth'), may hold values from 16 to 48, as said below
Outputs:
- row_scale: float32 [131072], P('row')
- col_scale: float32 [131072], P('col')
- scaled_tiles: float32 [4, 4, 96, 256, 256], P('row', 'col', 'depth')
The draws below stay inside these ranges and needn't reach their ends.
Inputs may be any that keep to these rules, and one draw needn't show every extreme that they name: `tile_rows`: every block row and every block column of the matrix holds a live tile; no block is listed twice among the live tiles of the two depth lists of one row and col index. `tile_count`: some device's list is full in every draw. `tiles`: entries in empty slots are ignored.
All inputs are finite; a program needn't handle non-finite values.
Results may differ from the reference program's by a relative error of at most 0.0001.
Values sent between devices are 32-bit elements; how exact they have to be, the bound alone decides.
A program may use at most 128 MiB of HBM per device.

```python
import math
import jax
import jax.numpy as jnp
from jax import lax

TILE = 256
RB_DEV = 128
ANCHORS = 16
SWEEPS = 4
SLOTS = 48
CB_DEV = 128
ROW_GROUPS = 4
COL_GROUPS = 4
DEPTH_SPLIT = 2


def pattern(key):
    base_key = jax.random.fold_in(key, 7)
    key_extra, key_order, key_count = jax.random.split(base_key, 3)
    groups_row = ROW_GROUPS
    groups_col = COL_GROUPS
    depths = DEPTH_SPLIT
    row_pos = jnp.arange(groups_row, dtype=jnp.int32)[:, None, None, None]
    col_pos = jnp.arange(groups_col, dtype=jnp.int32)[None, :, None, None]
    depth_pos = jnp.arange(depths, dtype=jnp.int32)[None, None, :, None]
    anchor_ids = jnp.arange(ANCHORS, dtype=jnp.int32)[None, None, None, :]
    shape_four = (groups_row, groups_col, depths, ANCHORS)
    anchor_cols = jnp.broadcast_to((row_pos * depths + depth_pos) * ANCHORS + anchor_ids, shape_four)
    extra_cols = jax.random.randint(key_extra, (groups_row, groups_col, depths, 2 * ANCHORS), 0, CB_DEV).astype(jnp.int32)
    all_cols = jnp.concatenate([anchor_cols, extra_cols], axis=3)
    window_start = col_pos * depths * ANCHORS
    anchor_spot = jnp.broadcast_to(window_start + depth_pos * ANCHORS + anchor_ids, shape_four)
    second_spot = jnp.broadcast_to(window_start + depths * ANCHORS + depth_pos * ANCHORS + anchor_ids, shape_four)
    third_spot = jnp.broadcast_to(window_start + depths * ANCHORS + (depths + depth_pos) * ANCHORS + anchor_ids, shape_four)
    spots = jnp.concatenate([anchor_spot, second_spot, third_spot], axis=3) % RB_DEV
    order_keys = jax.random.split(key_order, groups_row)
    row_order = jax.vmap(lambda one_key: jax.random.permutation(one_key, RB_DEV))(order_keys).astype(jnp.int32)
    flat_spots = spots.reshape(groups_row, groups_col * depths * SLOTS)
    all_rows = jnp.take_along_axis(row_order, flat_spots, axis=1)
    all_rows = all_rows.reshape(groups_row, groups_col, depths * SLOTS).astype(jnp.int32)
    all_cols = all_cols.reshape(groups_row, groups_col, depths * SLOTS).astype(jnp.int32)
    level = jax.random.randint(key_count, (groups_row, groups_col, depths), 0, 2 * ANCHORS + 1).astype(jnp.int32)
    extra = level * level * level // (4 * ANCHORS * ANCHORS)
    counts = ANCHORS + extra
    chosen = jax.random.randint(jax.random.fold_in(key_count, 1), (), 0, groups_row * groups_col * depths).astype(jnp.int32)
    flat_ids = jnp.arange(groups_row * groups_col * depths, dtype=jnp.int32).reshape(groups_row, groups_col, depths)
    counts = jnp.where(flat_ids == chosen, jnp.int32(SLOTS), counts).astype(jnp.int32)
    return (all_rows, all_cols, counts)


def draw_tile_rows(key, part):
    return pattern(key)[0]


def draw_tile_cols(key, part):
    return pattern(key)[1]


def draw_tile_count(key, part):
    return pattern(key)[2]


def draw_tiles(key, part):
    key_values, key_rowscale, key_colscale = jax.random.split(jax.random.fold_in(key, 11), 3)
    shape_all = (ROW_GROUPS, COL_GROUPS, DEPTH_SPLIT * SLOTS, TILE, TILE)
    shape_rowscale = (ROW_GROUPS, COL_GROUPS, DEPTH_SPLIT * SLOTS, TILE, 1)
    shape_colscale = (ROW_GROUPS, COL_GROUPS, DEPTH_SPLIT * SLOTS, 1, TILE)
    entries = jax.random.normal(key_values, shape_all, jnp.float32)
    reach = math.log(30.0)
    row_spread = jnp.exp(jax.random.uniform(key_rowscale, shape_rowscale, jnp.float32, 0.0, reach))
    col_spread = jnp.exp(jax.random.uniform(key_colscale, shape_colscale, jnp.float32, 0.0, reach))
    return (entries * row_spread * col_spread).astype(jnp.float32)


def setup_inputs(seed: int = 0) -> dict:
    arg_keys = jax.random.split(jax.random.key(seed), 5)
    tiles = draw_tiles(jax.random.fold_in(arg_keys[4], 71), 0)
    tile_rows = draw_tile_rows(jax.random.fold_in(arg_keys[4], 71), 0)
    tile_cols = draw_tile_cols(jax.random.fold_in(arg_keys[4], 71), 0)
    tile_count = draw_tile_count(jax.random.fold_in(arg_keys[4], 71), 0)
    return dict(tiles=tiles, tile_rows=tile_rows, tile_cols=tile_cols, tile_count=tile_count)


EPS = 1e-06

def reference(tiles, tile_rows, tile_cols, tile_count):
    groups_row = ROW_GROUPS
    groups_col = COL_GROUPS
    slot_total = DEPTH_SPLIT * SLOTS
    slot_ids = jnp.arange(slot_total, dtype=jnp.int32)
    depth_of = slot_ids // SLOTS
    within = slot_ids % SLOTS
    live_mask = within[None, None, :] < tile_count[:, :, depth_of]
    global_rows = (jnp.arange(groups_row, dtype=jnp.int32)[:, None, None] * RB_DEV + tile_rows).reshape(groups_row * groups_col, slot_total)
    global_cols = (jnp.arange(groups_col, dtype=jnp.int32)[None, :, None] * CB_DEV + tile_cols).reshape(groups_row * groups_col, slot_total)
    flat_tiles = tiles.reshape(groups_row * groups_col, slot_total, TILE, TILE)
    flat_live = live_mask.reshape(groups_row * groups_col, slot_total)
    row_factor = jnp.ones((groups_row * RB_DEV, TILE), jnp.float32)
    col_factor = jnp.ones((groups_col * CB_DEV, TILE), jnp.float32)

    def partials(row_now, col_now, summed):

        def one_group(items):
            block_values, row_index, col_index, alive = items
            scaled = block_values * row_now[row_index][:, :, None] * col_now[col_index][:, None, :]
            magnitude = jnp.where(alive[:, None, None], jnp.abs(scaled), jnp.float32(0.0))
            if summed:
                return (magnitude.sum(axis=2), magnitude.sum(axis=1))
            return (magnitude.max(axis=2), magnitude.max(axis=1))
        row_part, col_part = lax.map(one_group, (flat_tiles, global_rows, global_cols, flat_live))
        row_zero = jnp.zeros((groups_row * RB_DEV, TILE), jnp.float32)
        col_zero = jnp.zeros((groups_col * CB_DEV, TILE), jnp.float32)
        if summed:
            row_total = row_zero.at[global_rows.reshape(-1)].add(row_part.reshape(-1, TILE))
            col_total = col_zero.at[global_cols.reshape(-1)].add(col_part.reshape(-1, TILE))
        else:
            row_total = row_zero.at[global_rows.reshape(-1)].max(row_part.reshape(-1, TILE))
            col_total = col_zero.at[global_cols.reshape(-1)].max(col_part.reshape(-1, TILE))
        return (row_total, col_total)
    for sweep_index in range(SWEEPS):
        row_peak, col_peak = partials(row_factor, col_factor, False)
        row_factor = row_factor * lax.rsqrt(row_peak + EPS)
        col_factor = col_factor * lax.rsqrt(col_peak + EPS)
    row_mass, col_mass = partials(row_factor, col_factor, True)
    row_factor = row_factor * lax.rsqrt(row_mass + EPS)
    col_factor = col_factor * lax.rsqrt(col_mass + EPS)

    def final_group(items):
        block_values, row_index, col_index, alive = items
        scaled = block_values * row_factor[row_index][:, :, None] * col_factor[col_index][:, None, :]
        return jnp.where(alive[:, None, None], scaled, jnp.float32(0.0))
    scaled_tiles = lax.map(final_group, (flat_tiles, global_rows, global_cols, flat_live))
    scaled_tiles = scaled_tiles.reshape(groups_row, groups_col, slot_total, TILE, TILE)
    return (row_factor.reshape(-1), col_factor.reshape(-1), scaled_tiles)
```

```python
import functools

import jax
import jax.numpy as jnp
from jax import lax
from jax.experimental import pallas as pl
from jax.experimental.pallas import tpu as pltpu
from jax.sharding import PartitionSpec as P

RB_DEV = 128
ANCHORS = 16
SWEEPS = 4
EPS = 1e-06
MESH = pl.DeviceIdType.MESH
ROUNDS = SWEEPS + 1


def scale_kernel(
    rows, cols, count, tiles, r_out, c_out,
    mag, load_sem, r_fac, c_fac, row_part, col_part,
    row_acc, col_acc, row_half, col_half, row_comb, col_comb, row_got, col_got,
    row_s1, row_r1, col_s1, col_r1, row_s2, row_r2, col_s2, col_r2, row_sg, row_rg, col_sg, col_rg,
):
    depths = lax.axis_size("depth")
    me_d = lax.axis_index("depth")
    slots, size = tiles.shape[0], tiles.shape[1]
    lanes = 128
    live = count[0]

    def load(s):
        return pltpu.make_async_copy(tiles.at[s], mag.at[s], load_sem.at[s])

    @pl.loop(0, slots)
    def _(s):
        load(s).start()

    def peers(axis):
        n = lax.axis_size(axis)
        me = lax.axis_index(axis)
        return [(k, {axis: lax.rem(me + k, n)}) for k in range(1, n)]

    barrier = pltpu.get_barrier_semaphore()
    greeted = 0
    for axis in ("row", "col", "depth"):
        for _, dev in peers(axis):
            pl.semaphore_signal(barrier, inc=1, device_id=dev, device_id_type=MESH)
            greeted += 1
    pl.semaphore_wait(barrier, greeted)

    class Side:
        def __init__(self, axis, fac, acc, half, comb, got, s1, r1, s2, r2, sg, rg):
            self.axis, self.fac, self.acc, self.half, self.comb, self.got = axis, fac, acc, half, comb, got
            self.s1, self.r1, self.s2, self.r2, self.sg, self.rg = s1, r1, s2, r2, sg, rg
            self.hb = acc.shape[2]

        def pair_copies(self, t):
            return [
                pltpu.make_async_remote_copy(
                    src_ref=self.acc.at[t, dev["depth"]], dst_ref=self.half.at[t, k - 1],
                    send_sem=self.s1.at[t, k - 1], recv_sem=self.r1.at[t, k - 1],
                    device_id=dev, device_id_type=MESH)
                for k, dev in peers("depth")
            ]

        def group_copies(self, t):
            return [
                pltpu.make_async_remote_copy(
                    src_ref=self.comb.at[t], dst_ref=self.got.at[t, k - 1],
                    send_sem=self.sg.at[t, k - 1], recv_sem=self.rg.at[t, k - 1],
                    device_id=dev, device_id_type=MESH)
                for k, dev in peers(self.axis)
            ]

        def back_copies(self, t):
            return [
                pltpu.make_async_remote_copy(
                    src_ref=self.fac.at[t + 1, me_d], dst_ref=self.fac.at[t + 1, me_d],
                    send_sem=self.s2.at[t, k - 1], recv_sem=self.r2.at[t, k - 1],
                    device_id=dev, device_id_type=MESH)
                for k, dev in peers("depth")
            ]

        def start_pair(self, t):
            for c in self.pair_copies(t):
                c.start()

        def pair_to_group(self, t, op):
            for c in self.pair_copies(t):
                c.wait()
            value = self.acc[t, me_d]
            for k in range(self.half.shape[1]):
                value = op(value, self.half[t, k])
            self.comb[t] = value
            for c in self.group_copies(t):
                c.start()

        def group_to_back(self, t, op):
            for c in self.group_copies(t):
                c.wait()
            value = self.comb[t]
            for k in range(self.got.shape[1]):
                value = op(value, self.got[t, k])
            now = self.fac[t, me_d]
            self.fac[t + 1, me_d] = now * lax.rsqrt(now * value + EPS)
            for c in self.back_copies(t):
                c.start()

        def finish_back(self, t):
            for c in self.back_copies(t):
                c.wait()

    row = Side("col", r_fac, row_acc, row_half, row_comb, row_got, row_s1, row_r1, row_s2, row_r2, row_sg, row_rg)
    col = Side("row", c_fac, col_acc, col_half, col_comb, col_got, col_s1, col_r1, col_s2, col_r2, col_sg, col_rg)

    def spread(side, t, part, ids, summed):
        shape = side.acc.shape[2:]
        for d in range(depths):
            block = lax.broadcasted_iota(jnp.int32, shape, 0) + d * side.hb

            def add(s, acc):
                term = jnp.where(block == ids[s], part[s], jnp.float32(0.0))
                return acc + term if summed else jnp.maximum(acc, term)

            side.acc[t, d] = lax.fori_loop(0, slots, add, jnp.zeros(shape, jnp.float32), unroll=4)

    def factor(side, t, index):
        return side.fac[t, index // side.hb, pl.ds(index % side.hb, 1), :]

    def fold_rows(x, summed):
        chunks = [x[:, j:j + lanes] for j in range(0, size, lanes)]
        op = jnp.add if summed else jnp.maximum
        z = functools.reduce(op, chunks).T
        return z.sum(axis=0, keepdims=True) if summed else z.max(axis=0, keepdims=True)

    def fold_cols(x, summed):
        return x.sum(axis=0, keepdims=True) if summed else x.max(axis=0, keepdims=True)

    def col_pass(t, summed):
        @pl.loop(0, slots, unroll=2)
        def _(s):
            r = factor(row, t, rows[s])
            rt = jnp.broadcast_to(r, (lanes, size)).T
            for j in range(0, size, lanes):
                col_part[s, :, j:j + lanes] = fold_cols(mag[s, :, j:j + lanes] * rt, summed)

        spread(col, t, col_part, cols, summed)
        col.start_pair(t)

    def row_pass(t, summed):
        @pl.loop(0, slots, unroll=2)
        def _(s):
            c = factor(col, t, cols[s])
            row_part[s] = fold_rows(mag[s] * c, summed)

        spread(row, t, row_part, rows, summed)
        row.start_pair(t)

    r_fac[0] = jnp.ones(r_fac.shape[1:], jnp.float32)
    c_fac[0] = jnp.ones(c_fac.shape[1:], jnp.float32)

    @pl.loop(0, slots)
    def _(s):
        load(s).wait()
        u = jnp.where(s < live, jnp.abs(mag[s]), jnp.float32(0.0))
        mag[s] = u
        row_part[s] = fold_rows(u, False)
        col_part[s] = fold_cols(u, False)

    spread(col, 0, col_part, cols, False)
    col.start_pair(0)
    spread(row, 0, row_part, rows, False)
    row.start_pair(0)
    col.pair_to_group(0, jnp.maximum)
    row.pair_to_group(0, jnp.maximum)

    def step(t, op, next_summed, last):
        next_op = jnp.add if next_summed else jnp.maximum
        row.group_to_back(t, op)
        row.finish_back(t)
        if not last:
            col_pass(t + 1, next_summed)
        col.group_to_back(t, op)
        if not last:
            col.pair_to_group(t + 1, next_op)
        col.finish_back(t)
        if not last:
            row_pass(t + 1, next_summed)
            row.pair_to_group(t + 1, next_op)

    @pl.loop(0, SWEEPS - 1)
    def _(t):
        step(t, jnp.maximum, False, False)

    step(SWEEPS - 1, jnp.maximum, True, False)
    step(SWEEPS, jnp.add, False, True)
    r_out[...] = r_fac[ROUNDS]
    c_out[...] = c_fac[ROUNDS]


def final_kernel(rows, cols, count, tiles, r_fac, c_fac, out):
    group, size = tiles.shape[0], tiles.shape[1]
    lanes = 128
    base = pl.program_id(0) * group
    for k in range(group):
        s = base + k

        @pl.when(s < count[0])
        def _():
            r = r_fac[pl.ds(rows[s], 1), :]
            c = c_fac[pl.ds(cols[s], 1), :]
            rt = jnp.broadcast_to(r, (lanes, size)).T
            for j in range(0, size, lanes):
                out[k, :, j:j + lanes] = tiles[k, :, j:j + lanes] * rt * c[:, j:j + lanes]

        @pl.when(s >= count[0])
        def _():
            out[k] = jnp.zeros((size, size), jnp.float32)


def shards(tiles, tile_rows, tile_cols, tile_count):
    values = tiles[0, 0]
    rows = tile_rows.reshape(-1)
    cols = tile_cols.reshape(-1)
    count = tile_count.reshape(-1)
    slots, size = values.shape[0], values.shape[1]
    n_row, n_col, depths = lax.axis_size("row"), lax.axis_size("col"), lax.axis_size("depth")
    col_blocks = n_row * depths * ANCHORS
    rh, ch = RB_DEV // depths, col_blocks // depths
    f32 = jnp.float32
    dma = pltpu.SemaphoreType.DMA
    d1 = depths - 1
    smem = pl.BlockSpec(memory_space=pltpu.SMEM)
    vmem = pl.BlockSpec(memory_space=pltpu.VMEM)
    row_scale, col_scale = pl.pallas_call(
        scale_kernel,
        out_shape=(
            jax.ShapeDtypeStruct((depths, rh, size), f32),
            jax.ShapeDtypeStruct((depths, ch, size), f32),
        ),
        in_specs=[smem, smem, smem, pl.BlockSpec(memory_space=pl.ANY)],
        out_specs=(vmem, vmem),
        scratch_shapes=[
            pltpu.VMEM((slots, size, size), f32),
            dma((slots,)),
            pltpu.VMEM((ROUNDS + 1, depths, rh, size), f32),
            pltpu.VMEM((ROUNDS + 1, depths, ch, size), f32),
            pltpu.VMEM((slots, 1, size), f32),
            pltpu.VMEM((slots, 1, size), f32),
            pltpu.VMEM((ROUNDS, depths, rh, size), f32),
            pltpu.VMEM((ROUNDS, depths, ch, size), f32),
            pltpu.VMEM((ROUNDS, d1, rh, size), f32),
            pltpu.VMEM((ROUNDS, d1, ch, size), f32),
            pltpu.VMEM((ROUNDS, rh, size), f32),
            pltpu.VMEM((ROUNDS, ch, size), f32),
            pltpu.VMEM((ROUNDS, n_col - 1, rh, size), f32),
            pltpu.VMEM((ROUNDS, n_row - 1, ch, size), f32),
            dma((ROUNDS, d1)), dma((ROUNDS, d1)), dma((ROUNDS, d1)), dma((ROUNDS, d1)),
            dma((ROUNDS, d1)), dma((ROUNDS, d1)), dma((ROUNDS, d1)), dma((ROUNDS, d1)),
            dma((ROUNDS, n_col - 1)), dma((ROUNDS, n_col - 1)),
            dma((ROUNDS, n_row - 1)), dma((ROUNDS, n_row - 1)),
        ],
        compiler_params=pltpu.CompilerParams(
            collective_id=0, has_side_effects=True, vmem_limit_bytes=40 * 2**20
        ),
        name="equilibrate",
    )(rows, cols, count, values)
    row_scale = row_scale.reshape(depths * rh, size)
    col_scale = col_scale.reshape(depths * ch, size)

    group = next(g for g in (4, 3, 2, 1) if slots % g == 0)
    whole = lambda shape: pl.BlockSpec(shape, lambda g, *_: (0, 0))

    def in_map(g, rows, cols, count):
        return (jnp.minimum(g, jnp.maximum(count[0] - 1, 0) // group), 0, 0)

    scaled = pl.pallas_call(
        final_kernel,
        grid_spec=pltpu.PrefetchScalarGridSpec(
            num_scalar_prefetch=3,
            grid=(slots // group,),
            in_specs=[
                pl.BlockSpec((group, size, size), in_map),
                whole(row_scale.shape),
                whole(col_scale.shape),
            ],
            out_specs=pl.BlockSpec((group, size, size), lambda g, *_: (g, 0, 0)),
        ),
        out_shape=jax.ShapeDtypeStruct(values.shape, f32),
        name="scale_tiles",
    )(rows, cols, count, values, row_scale, col_scale)
    return (row_scale.reshape(-1), col_scale.reshape(-1), scaled[None, None])


def solution(mesh):
    in_specs = (
        P("row", "col", "depth", None, None),
        P("row", "col", "depth"),
        P("row", "col", "depth"),
        P("row", "col", "depth"),
    )
    out_specs = (P("row"), P("col"), P("row", "col", "depth", None, None))
    return jax.shard_map(shards, mesh=mesh, in_specs=in_specs, out_specs=out_specs, check_vma=False)
```

```python
import functools

import jax
import jax.numpy as jnp
from jax import lax
from jax.experimental import pallas as pl
from jax.experimental.pallas import tpu as pltpu
from jax.sharding import PartitionSpec as P

RB_DEV = 128
ANCHORS = 16
SWEEPS = 4
EPS = 1e-06
UNROLL = 8
MESH = pl.DeviceIdType.MESH
ROUNDS = SWEEPS + 1


def scale_kernel(
    rows, cols, count, tiles, r_out, c_out,
    mag, mag_t, load_sem, r_fac, c_fac, row_part, col_part,
    row_acc, col_acc, row_half, col_half, row_comb, col_comb, row_got, col_got,
    row_s1, row_r1, col_s1, col_r1, row_s2, row_r2, col_s2, col_r2, row_sg, row_rg, col_sg, col_rg,
):
    depths = lax.axis_size("depth")
    me_d = lax.axis_index("depth")
    slots, size = tiles.shape[0], tiles.shape[1]
    lanes = 128
    live = count[0]

    def load(s):
        return pltpu.make_async_copy(tiles.at[s], mag.at[s], load_sem.at[s])

    @pl.loop(0, slots)
    def _(s):
        load(s).start()

    def peers(axis):
        n = lax.axis_size(axis)
        me = lax.axis_index(axis)
        return [(k, {axis: lax.rem(me + k, n)}) for k in range(1, n)]

    barrier = pltpu.get_barrier_semaphore()
    greeted = 0
    for axis in ("row", "col", "depth"):
        for _, dev in peers(axis):
            pl.semaphore_signal(barrier, inc=1, device_id=dev, device_id_type=MESH)
            greeted += 1
    pl.semaphore_wait(barrier, greeted)

    class Side:
        def __init__(self, axis, fac, acc, half, comb, got, s1, r1, s2, r2, sg, rg):
            self.axis, self.fac, self.acc, self.half, self.comb, self.got = axis, fac, acc, half, comb, got
            self.s1, self.r1, self.s2, self.r2, self.sg, self.rg = s1, r1, s2, r2, sg, rg
            self.hb = acc.shape[2]

        def pair_copies(self, t):
            return [
                pltpu.make_async_remote_copy(
                    src_ref=self.acc.at[t, dev["depth"]], dst_ref=self.half.at[t, k - 1],
                    send_sem=self.s1.at[t, k - 1], recv_sem=self.r1.at[t, k - 1],
                    device_id=dev, device_id_type=MESH)
                for k, dev in peers("depth")
            ]

        def group_copies(self, t):
            return [
                pltpu.make_async_remote_copy(
                    src_ref=self.comb.at[t], dst_ref=self.got.at[t, k - 1],
                    send_sem=self.sg.at[t, k - 1], recv_sem=self.rg.at[t, k - 1],
                    device_id=dev, device_id_type=MESH)
                for k, dev in peers(self.axis)
            ]

        def back_copies(self, t):
            return [
                pltpu.make_async_remote_copy(
                    src_ref=self.fac.at[t + 1, me_d], dst_ref=self.fac.at[t + 1, me_d],
                    send_sem=self.s2.at[t, k - 1], recv_sem=self.r2.at[t, k - 1],
                    device_id=dev, device_id_type=MESH)
                for k, dev in peers("depth")
            ]

        def start_pair(self, t):
            for c in self.pair_copies(t):
                c.start()

        def pair_to_group(self, t, op):
            for c in self.pair_copies(t):
                c.wait()
            value = self.acc[t, me_d]
            for k in range(self.half.shape[1]):
                value = op(value, self.half[t, k])
            self.comb[t] = value
            for c in self.group_copies(t):
                c.start()

        def group_to_back(self, t, op):
            for c in self.group_copies(t):
                c.wait()
            value = self.comb[t]
            for k in range(self.got.shape[1]):
                value = op(value, self.got[t, k])
            now = self.fac[t, me_d]
            self.fac[t + 1, me_d] = now * lax.rsqrt(now * value + EPS)
            for c in self.back_copies(t):
                c.start()

        def finish_back(self, t):
            for c in self.back_copies(t):
                c.wait()

    row = Side("col", r_fac, row_acc, row_half, row_comb, row_got, row_s1, row_r1, row_s2, row_r2, row_sg, row_rg)
    col = Side("row", c_fac, col_acc, col_half, col_comb, col_got, col_s1, col_r1, col_s2, col_r2, col_sg, col_rg)

    def spread(side, t, part, ids, summed):
        shape = side.acc.shape[2:]
        for d in range(depths):
            block = lax.broadcasted_iota(jnp.int32, shape, 0) + d * side.hb

            def add(s, acc):
                term = jnp.where(block == ids[s], part[s], jnp.float32(0.0))
                return acc + term if summed else jnp.maximum(acc, term)

            side.acc[t, d] = lax.fori_loop(0, slots, add, jnp.zeros(shape, jnp.float32), unroll=4)

    def factor(side, t, index):
        return side.fac[t, index // side.hb, pl.ds(index % side.hb, 1), :]

    def down(f):
        return jnp.broadcast_to(f, (lanes, size)).T

    def fold(x, summed):
        return x.sum(axis=0, keepdims=True) if summed else x.max(axis=0, keepdims=True)

    def half_pass(other, side, values, part, here, there, t, summed):
        @pl.loop(0, slots, unroll=UNROLL)
        def _(s):
            f = down(factor(other, t, there[s]))
            for j in range(0, size, lanes):
                part[s, :, j:j + lanes] = fold(values[s, :, j:j + lanes] * f, summed)

        spread(side, t, part, here, summed)
        side.start_pair(t)

    def col_pass(t, summed):
        half_pass(row, col, mag, col_part, cols, rows, t, summed)

    def row_pass(t, summed):
        half_pass(col, row, mag_t, row_part, rows, cols, t, summed)

    r_fac[0] = jnp.ones(r_fac.shape[1:], jnp.float32)
    c_fac[0] = jnp.ones(c_fac.shape[1:], jnp.float32)

    @pl.loop(0, slots, unroll=2)
    def _(s):
        load(s).wait()
        u = jnp.where(s < live, jnp.abs(mag[s]), jnp.float32(0.0))
        mag[s] = u
        col_part[s] = fold(u, False)
        ut = u.T
        mag_t[s] = ut
        row_part[s] = fold(ut, False)

    spread(col, 0, col_part, cols, False)
    col.start_pair(0)
    spread(row, 0, row_part, rows, False)
    row.start_pair(0)
    col.pair_to_group(0, jnp.maximum)
    row.pair_to_group(0, jnp.maximum)

    def step(t, op, next_summed, last):
        next_op = jnp.add if next_summed else jnp.maximum
        row.group_to_back(t, op)
        row.finish_back(t)
        if not last:
            col_pass(t + 1, next_summed)
        col.group_to_back(t, op)
        if not last:
            col.pair_to_group(t + 1, next_op)
        col.finish_back(t)
        if not last:
            row_pass(t + 1, next_summed)
            row.pair_to_group(t + 1, next_op)

    @pl.loop(0, SWEEPS - 1)
    def _(t):
        step(t, jnp.maximum, False, False)

    step(SWEEPS - 1, jnp.maximum, True, False)
    step(SWEEPS, jnp.add, False, True)
    r_out[...] = r_fac[ROUNDS]
    c_out[...] = c_fac[ROUNDS]


def final_kernel(rows, cols, count, tiles, r_fac, c_fac, out):
    group, size = tiles.shape[0], tiles.shape[1]
    lanes = 128
    base = pl.program_id(0) * group

    @pl.when(base < count[0])
    def _():
        for k in range(group):
            s = base + k
            r = jnp.where(s < count[0], r_fac[pl.ds(rows[s], 1), :], jnp.float32(0.0))
            c = c_fac[pl.ds(cols[s], 1), :]
            rt = jnp.broadcast_to(r, (lanes, size)).T
            for j in range(0, size, lanes):
                out[k, :, j:j + lanes] = tiles[k, :, j:j + lanes] * rt * c[:, j:j + lanes]

    @pl.when(base >= count[0])
    def _():
        out[...] = jnp.zeros_like(out)


def shards(tiles, tile_rows, tile_cols, tile_count):
    values = tiles[0, 0]
    rows = tile_rows.reshape(-1)
    cols = tile_cols.reshape(-1)
    count = tile_count.reshape(-1)
    slots, size = values.shape[0], values.shape[1]
    n_row, n_col, depths = lax.axis_size("row"), lax.axis_size("col"), lax.axis_size("depth")
    col_blocks = n_row * depths * ANCHORS
    rh, ch = RB_DEV // depths, col_blocks // depths
    f32 = jnp.float32
    dma = pltpu.SemaphoreType.DMA
    d1 = depths - 1
    smem = pl.BlockSpec(memory_space=pltpu.SMEM)
    vmem = pl.BlockSpec(memory_space=pltpu.VMEM)
    row_scale, col_scale = pl.pallas_call(
        scale_kernel,
        out_shape=(
            jax.ShapeDtypeStruct((depths, rh, size), f32),
            jax.ShapeDtypeStruct((depths, ch, size), f32),
        ),
        in_specs=[smem, smem, smem, pl.BlockSpec(memory_space=pl.ANY)],
        out_specs=(vmem, vmem),
        scratch_shapes=[
            pltpu.VMEM((slots, size, size), f32),
            pltpu.VMEM((slots, size, size), f32),
            dma((slots,)),
            pltpu.VMEM((ROUNDS + 1, depths, rh, size), f32),
            pltpu.VMEM((ROUNDS + 1, depths, ch, size), f32),
            pltpu.VMEM((slots, 1, size), f32),
            pltpu.VMEM((slots, 1, size), f32),
            pltpu.VMEM((ROUNDS, depths, rh, size), f32),
            pltpu.VMEM((ROUNDS, depths, ch, size), f32),
            pltpu.VMEM((ROUNDS, d1, rh, size), f32),
            pltpu.VMEM((ROUNDS, d1, ch, size), f32),
            pltpu.VMEM((ROUNDS, rh, size), f32),
            pltpu.VMEM((ROUNDS, ch, size), f32),
            pltpu.VMEM((ROUNDS, n_col - 1, rh, size), f32),
            pltpu.VMEM((ROUNDS, n_row - 1, ch, size), f32),
            dma((ROUNDS, d1)), dma((ROUNDS, d1)), dma((ROUNDS, d1)), dma((ROUNDS, d1)),
            dma((ROUNDS, d1)), dma((ROUNDS, d1)), dma((ROUNDS, d1)), dma((ROUNDS, d1)),
            dma((ROUNDS, n_col - 1)), dma((ROUNDS, n_col - 1)),
            dma((ROUNDS, n_row - 1)), dma((ROUNDS, n_row - 1)),
        ],
        compiler_params=pltpu.CompilerParams(
            collective_id=0, has_side_effects=True, vmem_limit_bytes=60 * 2**20
        ),
        name="equilibrate",
    )(rows, cols, count, values)
    row_scale = row_scale.reshape(depths * rh, size)
    col_scale = col_scale.reshape(depths * ch, size)

    group = next(g for g in (4, 3, 2, 1) if slots % g == 0)
    whole = lambda shape: pl.BlockSpec(shape, lambda g, *_: (0, 0))

    def in_map(g, rows, cols, count):
        return (jnp.minimum(g, jnp.maximum(count[0] - 1, 0) // group), 0, 0)

    scaled = pl.pallas_call(
        final_kernel,
        grid_spec=pltpu.PrefetchScalarGridSpec(
            num_scalar_prefetch=3,
            grid=(slots // group,),
            in_specs=[
                pl.BlockSpec((group, size, size), in_map),
                whole(row_scale.shape),
                whole(col_scale.shape),
            ],
            out_specs=pl.BlockSpec((group, size, size), lambda g, *_: (g, 0, 0)),
        ),
        out_shape=jax.ShapeDtypeStruct(values.shape, f32),
        name="scale_tiles",
    )(rows, cols, count, values, row_scale, col_scale)
    return (row_scale.reshape(-1), col_scale.reshape(-1), scaled[None, None])


def solution(mesh):
    in_specs = (
        P("row", "col", "depth", None, None),
        P("row", "col", "depth"),
        P("row", "col", "depth"),
        P("row", "col", "depth"),
    )
    out_specs = (P("row"), P("col"), P("row", "col", "depth", None, None))
    return jax.shard_map(shards, mesh=mesh, in_specs=in_specs, out_specs=out_specs, check_vma=False)
```

```python
import functools

import jax
import jax.numpy as jnp
from jax import lax
from jax.experimental import pallas as pl
from jax.experimental.pallas import tpu as pltpu
from jax.sharding import PartitionSpec as P

RB_DEV = 128
ANCHORS = 16
SWEEPS = 4
EPS = 1e-06
UNROLL = 8
GROUP = 4
MESH = pl.DeviceIdType.MESH
ROUNDS = SWEEPS + 1


def scale_kernel(
    rows, cols, count, tiles, r_out, c_out,
    mag, mag_t, load_sem, r_fac, c_fac, row_part, col_part,
    row_acc, col_acc, row_half, col_half, row_comb, col_comb, row_got, col_got,
    row_s1, row_r1, col_s1, col_r1, row_s2, row_r2, col_s2, col_r2, row_sg, row_rg, col_sg, col_rg,
):
    depths = lax.axis_size("depth")
    me_d = lax.axis_index("depth")
    slots, size = tiles.shape[0], tiles.shape[1]
    lanes = 128
    live = count[0]

    def load(s):
        return pltpu.make_async_copy(tiles.at[s], mag.at[s], load_sem.at[s])

    @pl.loop(0, slots)
    def _(s):
        load(s).start()

    def peers(axis):
        n = lax.axis_size(axis)
        me = lax.axis_index(axis)
        return [(k, {axis: lax.rem(me + k, n)}) for k in range(1, n)]

    barrier = pltpu.get_barrier_semaphore()
    greeted = 0
    for axis in ("row", "col", "depth"):
        for _, dev in peers(axis):
            pl.semaphore_signal(barrier, inc=1, device_id=dev, device_id_type=MESH)
            greeted += 1
    pl.semaphore_wait(barrier, greeted)

    class Side:
        def __init__(self, axis, fac, acc, half, comb, got, s1, r1, s2, r2, sg, rg):
            self.axis, self.fac, self.acc, self.half, self.comb, self.got = axis, fac, acc, half, comb, got
            self.s1, self.r1, self.s2, self.r2, self.sg, self.rg = s1, r1, s2, r2, sg, rg
            self.hb = acc.shape[2]

        def pair_copies(self, t):
            return [
                pltpu.make_async_remote_copy(
                    src_ref=self.acc.at[t, dev["depth"]], dst_ref=self.half.at[t, k - 1],
                    send_sem=self.s1.at[t, k - 1], recv_sem=self.r1.at[t, k - 1],
                    device_id=dev, device_id_type=MESH)
                for k, dev in peers("depth")
            ]

        def group_copies(self, t):
            return [
                pltpu.make_async_remote_copy(
                    src_ref=self.comb.at[t], dst_ref=self.got.at[t, k - 1],
                    send_sem=self.sg.at[t, k - 1], recv_sem=self.rg.at[t, k - 1],
                    device_id=dev, device_id_type=MESH)
                for k, dev in peers(self.axis)
            ]

        def back_copies(self, t):
            return [
                pltpu.make_async_remote_copy(
                    src_ref=self.fac.at[t + 1, me_d], dst_ref=self.fac.at[t + 1, me_d],
                    send_sem=self.s2.at[t, k - 1], recv_sem=self.r2.at[t, k - 1],
                    device_id=dev, device_id_type=MESH)
                for k, dev in peers("depth")
            ]

        def start_pair(self, t):
            for c in self.pair_copies(t):
                c.start()

        def pair_to_group(self, t, op):
            for c in self.pair_copies(t):
                c.wait()
            value = self.acc[t, me_d]
            for k in range(self.half.shape[1]):
                value = op(value, self.half[t, k])
            self.comb[t] = value
            for c in self.group_copies(t):
                c.start()

        def group_to_back(self, t, op):
            for c in self.group_copies(t):
                c.wait()
            value = self.comb[t]
            for k in range(self.got.shape[1]):
                value = op(value, self.got[t, k])
            now = self.fac[t, me_d]
            self.fac[t + 1, me_d] = now * lax.rsqrt(now * value + EPS)
            for c in self.back_copies(t):
                c.start()

        def finish_back(self, t):
            for c in self.back_copies(t):
                c.wait()

    row = Side("col", r_fac, row_acc, row_half, row_comb, row_got, row_s1, row_r1, row_s2, row_r2, row_sg, row_rg)
    col = Side("row", c_fac, col_acc, col_half, col_comb, col_got, col_s1, col_r1, col_s2, col_r2, col_sg, col_rg)

    def spread(side, t, part, ids, summed):
        shape = side.acc.shape[2:]
        for d in range(depths):
            block = lax.broadcasted_iota(jnp.int32, shape, 0) + d * side.hb

            def add(s, acc):
                term = jnp.where(block == ids[s], part[s], jnp.float32(0.0))
                return acc + term if summed else jnp.maximum(acc, term)

            side.acc[t, d] = lax.fori_loop(0, slots, add, jnp.zeros(shape, jnp.float32), unroll=4)

    def factor(side, t, index):
        return side.fac[t, index // side.hb, pl.ds(index % side.hb, 1), :]

    def down(f):
        return jnp.broadcast_to(f, (lanes, size)).T

    def fold(x, summed):
        return x.sum(axis=0, keepdims=True) if summed else x.max(axis=0, keepdims=True)

    def half_pass(other, side, values, part, here, there, t, summed):
        @pl.loop(0, slots, unroll=UNROLL)
        def _(s):
            f = down(factor(other, t, there[s]))
            for j in range(0, size, lanes):
                part[s, :, j:j + lanes] = fold(values[s, :, j:j + lanes] * f, summed)

        spread(side, t, part, here, summed)
        side.start_pair(t)

    def col_pass(t, summed):
        half_pass(row, col, mag, col_part, cols, rows, t, summed)

    def row_pass(t, summed):
        half_pass(col, row, mag_t, row_part, rows, cols, t, summed)

    r_fac[0] = jnp.ones(r_fac.shape[1:], jnp.float32)
    c_fac[0] = jnp.ones(c_fac.shape[1:], jnp.float32)

    @pl.loop(0, slots, unroll=2)
    def _(s):
        load(s).wait()
        u = jnp.where(s < live, jnp.abs(mag[s]), jnp.float32(0.0))
        mag[s] = u
        col_part[s] = fold(u, False)
        wide = functools.reduce(jnp.maximum, [u[:, j:j + lanes] for j in range(0, size, lanes)])
        row_part[s] = fold(wide.T, False)

    spread(col, 0, col_part, cols, False)
    col.start_pair(0)
    spread(row, 0, row_part, rows, False)
    row.start_pair(0)
    col.pair_to_group(0, jnp.maximum)
    row.pair_to_group(0, jnp.maximum)

    @pl.loop(0, slots, unroll=4)
    def _(s):
        mag_t[s] = mag[s].T

    def step(t, op, next_summed, last):
        next_op = jnp.add if next_summed else jnp.maximum
        row.group_to_back(t, op)
        row.finish_back(t)
        if not last:
            col_pass(t + 1, next_summed)
        col.group_to_back(t, op)
        if not last:
            col.pair_to_group(t + 1, next_op)
        col.finish_back(t)
        if not last:
            row_pass(t + 1, next_summed)
            row.pair_to_group(t + 1, next_op)

    @pl.loop(0, SWEEPS - 1)
    def _(t):
        step(t, jnp.maximum, False, False)

    step(SWEEPS - 1, jnp.maximum, True, False)
    step(SWEEPS, jnp.add, False, True)
    r_out[...] = r_fac[ROUNDS]
    c_out[...] = c_fac[ROUNDS]


def final_kernel(rows, cols, count, tiles, r_fac, c_fac, out, held, made, zero, in_sem, out_sem):
    slots, size = tiles.shape[0], tiles.shape[1]
    group = GROUP if slots % GROUP == 0 else 1
    lanes = 128
    live = count[0]

    def load(s):
        return pltpu.make_async_copy(tiles.at[s], held.at[s], in_sem.at[s])

    def store(s):
        return pltpu.make_async_copy(made.at[s], out.at[s], out_sem.at[s])

    @pl.loop(0, slots)
    def _(s):
        @pl.when(s // group * group < live)
        def _():
            load(s).start()

    zero[...] = jnp.zeros_like(zero)

    @pl.loop(0, slots // group)
    def _(g):
        base = g * group

        @pl.when(base >= live)
        def _():
            for k in range(group):
                pltpu.make_async_copy(zero, out.at[base + k], out_sem.at[base + k]).start()

    @pl.loop(0, slots // group)
    def _(g):
        base = g * group

        @pl.when(base < live)
        def _():
            for k in range(group):
                load(base + k).wait()
            for k in range(group):
                s = base + k
                r = jnp.where(s < live, r_fac[pl.ds(rows[s], 1), :], jnp.float32(0.0))
                c = c_fac[pl.ds(cols[s], 1), :]
                rt = jnp.broadcast_to(r, (lanes, size)).T
                for j in range(0, size, lanes):
                    made[s, :, j:j + lanes] = held[s, :, j:j + lanes] * rt * c[:, j:j + lanes]
            for k in range(group):
                store(base + k).start()

    @pl.loop(0, slots)
    def _(s):
        store(s).wait()


def shards(tiles, tile_rows, tile_cols, tile_count):
    values = tiles[0, 0]
    rows = tile_rows.reshape(-1)
    cols = tile_cols.reshape(-1)
    count = tile_count.reshape(-1)
    slots, size = values.shape[0], values.shape[1]
    n_row, n_col, depths = lax.axis_size("row"), lax.axis_size("col"), lax.axis_size("depth")
    col_blocks = n_row * depths * ANCHORS
    rh, ch = RB_DEV // depths, col_blocks // depths
    f32 = jnp.float32
    dma = pltpu.SemaphoreType.DMA
    d1 = depths - 1
    smem = pl.BlockSpec(memory_space=pltpu.SMEM)
    vmem = pl.BlockSpec(memory_space=pltpu.VMEM)
    row_scale, col_scale = pl.pallas_call(
        scale_kernel,
        out_shape=(
            jax.ShapeDtypeStruct((depths, rh, size), f32),
            jax.ShapeDtypeStruct((depths, ch, size), f32),
        ),
        in_specs=[smem, smem, smem, pl.BlockSpec(memory_space=pl.ANY)],
        out_specs=(vmem, vmem),
        scratch_shapes=[
            pltpu.VMEM((slots, size, size), f32),
            pltpu.VMEM((slots, size, size), f32),
            dma((slots,)),
            pltpu.VMEM((ROUNDS + 1, depths, rh, size), f32),
            pltpu.VMEM((ROUNDS + 1, depths, ch, size), f32),
            pltpu.VMEM((slots, 1, size), f32),
            pltpu.VMEM((slots, 1, size), f32),
            pltpu.VMEM((ROUNDS, depths, rh, size), f32),
            pltpu.VMEM((ROUNDS, depths, ch, size), f32),
            pltpu.VMEM((ROUNDS, d1, rh, size), f32),
            pltpu.VMEM((ROUNDS, d1, ch, size), f32),
            pltpu.VMEM((ROUNDS, rh, size), f32),
            pltpu.VMEM((ROUNDS, ch, size), f32),
            pltpu.VMEM((ROUNDS, n_col - 1, rh, size), f32),
            pltpu.VMEM((ROUNDS, n_row - 1, ch, size), f32),
            dma((ROUNDS, d1)), dma((ROUNDS, d1)), dma((ROUNDS, d1)), dma((ROUNDS, d1)),
            dma((ROUNDS, d1)), dma((ROUNDS, d1)), dma((ROUNDS, d1)), dma((ROUNDS, d1)),
            dma((ROUNDS, n_col - 1)), dma((ROUNDS, n_col - 1)),
            dma((ROUNDS, n_row - 1)), dma((ROUNDS, n_row - 1)),
        ],
        compiler_params=pltpu.CompilerParams(
            collective_id=0, has_side_effects=True, vmem_limit_bytes=60 * 2**20
        ),
        name="equilibrate",
    )(rows, cols, count, values)
    row_scale = row_scale.reshape(depths * rh, size)
    col_scale = col_scale.reshape(depths * ch, size)

    scaled = pl.pallas_call(
        final_kernel,
        in_specs=[smem, smem, smem, pl.BlockSpec(memory_space=pl.ANY), vmem, vmem],
        out_specs=pl.BlockSpec(memory_space=pl.ANY),
        out_shape=jax.ShapeDtypeStruct(values.shape, f32),
        scratch_shapes=[
            pltpu.VMEM(values.shape, f32),
            pltpu.VMEM(values.shape, f32),
            pltpu.VMEM((size, size), f32),
            dma((slots,)),
            dma((slots,)),
        ],
        compiler_params=pltpu.CompilerParams(vmem_limit_bytes=60 * 2**20),
        name="scale_tiles",
    )(rows, cols, count, values, row_scale, col_scale)
    return (row_scale.reshape(-1), col_scale.reshape(-1), scaled[None, None])


def solution(mesh):
    in_specs = (
        P("row", "col", "depth", None, None),
        P("row", "col", "depth"),
        P("row", "col", "depth"),
        P("row", "col", "depth"),
    )
    out_specs = (P("row"), P("col"), P("row", "col", "depth", None, None))
    return jax.shard_map(shards, mesh=mesh, in_specs=in_specs, out_specs=out_specs, check_vma=False)
```

```python
import functools

import jax
import jax.numpy as jnp
from jax import lax
from jax.experimental import pallas as pl
from jax.experimental.pallas import tpu as pltpu
from jax.sharding import PartitionSpec as P

RB_DEV = 128
ANCHORS = 16
SWEEPS = 4
EPS = 1e-06
UNROLL = 16
GROUP = 4
MESH = pl.DeviceIdType.MESH
ROUNDS = SWEEPS + 1


def scale_kernel(
    rows, cols, count, tiles, r_out, c_out,
    mag, mag_t, load_sem, r_fac, c_fac, row_part, col_part,
    row_acc, col_acc, row_half, col_half, row_comb, col_comb, row_got, col_got,
    row_s1, row_r1, col_s1, col_r1, row_s2, row_r2, col_s2, col_r2, row_sg, row_rg, col_sg, col_rg,
):
    depths = lax.axis_size("depth")
    me_d = lax.axis_index("depth")
    slots, size = tiles.shape[0], tiles.shape[1]
    lanes = 128
    live = count[0]

    def load(s):
        return pltpu.make_async_copy(tiles.at[s], mag.at[s], load_sem.at[s])

    @pl.loop(0, slots)
    def _(s):
        load(s).start()

    def peers(axis):
        n = lax.axis_size(axis)
        me = lax.axis_index(axis)
        return [(k, {axis: lax.rem(me + k, n)}) for k in range(1, n)]

    barrier = pltpu.get_barrier_semaphore()
    greeted = 0
    for axis in ("row", "col", "depth"):
        for _, dev in peers(axis):
            pl.semaphore_signal(barrier, inc=1, device_id=dev, device_id_type=MESH)
            greeted += 1
    pl.semaphore_wait(barrier, greeted)

    class Side:
        def __init__(self, axis, fac, acc, half, comb, got, s1, r1, s2, r2, sg, rg):
            self.axis, self.fac, self.acc, self.half, self.comb, self.got = axis, fac, acc, half, comb, got
            self.s1, self.r1, self.s2, self.r2, self.sg, self.rg = s1, r1, s2, r2, sg, rg
            self.hb = acc.shape[2]

        def pair_copies(self, t):
            return [
                pltpu.make_async_remote_copy(
                    src_ref=self.acc.at[t, dev["depth"]], dst_ref=self.half.at[t, k - 1],
                    send_sem=self.s1.at[t, k - 1], recv_sem=self.r1.at[t, k - 1],
                    device_id=dev, device_id_type=MESH)
                for k, dev in peers("depth")
            ]

        def group_copies(self, t):
            return [
                pltpu.make_async_remote_copy(
                    src_ref=self.comb.at[t], dst_ref=self.got.at[t, k - 1],
                    send_sem=self.sg.at[t, k - 1], recv_sem=self.rg.at[t, k - 1],
                    device_id=dev, device_id_type=MESH)
                for k, dev in peers(self.axis)
            ]

        def back_copies(self, t):
            return [
                pltpu.make_async_remote_copy(
                    src_ref=self.fac.at[t + 1, me_d], dst_ref=self.fac.at[t + 1, me_d],
                    send_sem=self.s2.at[t, k - 1], recv_sem=self.r2.at[t, k - 1],
                    device_id=dev, device_id_type=MESH)
                for k, dev in peers("depth")
            ]

        def start_pair(self, t):
            for c in self.pair_copies(t):
                c.start()

        def pair_to_group(self, t, op):
            for c in self.pair_copies(t):
                c.wait()
            value = self.acc[t, me_d]
            for k in range(self.half.shape[1]):
                value = op(value, self.half[t, k])
            self.comb[t] = value
            for c in self.group_copies(t):
                c.start()

        def group_to_back(self, t, op):
            for c in self.group_copies(t):
                c.wait()
            value = self.comb[t]
            for k in range(self.got.shape[1]):
                value = op(value, self.got[t, k])
            now = self.fac[t, me_d]
            self.fac[t + 1, me_d] = now * lax.rsqrt(now * value + EPS)
            for c in self.back_copies(t):
                c.start()

        def finish_back(self, t):
            for c in self.back_copies(t):
                c.wait()

    row = Side("col", r_fac, row_acc, row_half, row_comb, row_got, row_s1, row_r1, row_s2, row_r2, row_sg, row_rg)
    col = Side("row", c_fac, col_acc, col_half, col_comb, col_got, col_s1, col_r1, col_s2, col_r2, col_sg, col_rg)

    def spread(side, t, part, ids, summed):
        shape = side.acc.shape[2:]
        for d in range(depths):
            block = lax.broadcasted_iota(jnp.int32, shape, 0) + d * side.hb

            def add(s, acc):
                term = jnp.where(block == ids[s], part[s], jnp.float32(0.0))
                return acc + term if summed else jnp.maximum(acc, term)

            side.acc[t, d] = lax.fori_loop(0, slots, add, jnp.zeros(shape, jnp.float32), unroll=8)

    def factor(side, t, index):
        return side.fac[t, index // side.hb, pl.ds(index % side.hb, 1), :]

    def down(f):
        return jnp.broadcast_to(f, (lanes, size)).T

    def fold(x, summed):
        return x.sum(axis=0, keepdims=True) if summed else x.max(axis=0, keepdims=True)

    def half_pass(other, side, values, part, here, there, t, summed):
        @pl.loop(0, slots, unroll=UNROLL)
        def _(s):
            f = down(factor(other, t, there[s]))
            for j in range(0, size, lanes):
                part[s, :, j:j + lanes] = fold(values[s, :, j:j + lanes] * f, summed)

        spread(side, t, part, here, summed)
        side.start_pair(t)

    def col_pass(t, summed):
        half_pass(row, col, mag, col_part, cols, rows, t, summed)

    def row_pass(t, summed):
        half_pass(col, row, mag_t, row_part, rows, cols, t, summed)

    r_fac[0] = jnp.ones(r_fac.shape[1:], jnp.float32)
    c_fac[0] = jnp.ones(c_fac.shape[1:], jnp.float32)

    @pl.loop(0, slots, unroll=2)
    def _(s):
        load(s).wait()
        u = jnp.where(s < live, jnp.abs(mag[s]), jnp.float32(0.0))
        mag[s] = u
        col_part[s] = fold(u, False)
        wide = functools.reduce(jnp.maximum, [u[:, j:j + lanes] for j in range(0, size, lanes)])
        row_part[s] = fold(wide.T, False)

    spread(col, 0, col_part, cols, False)
    col.start_pair(0)
    spread(row, 0, row_part, rows, False)
    row.start_pair(0)
    col.pair_to_group(0, jnp.maximum)
    row.pair_to_group(0, jnp.maximum)

    @pl.loop(0, slots, unroll=8)
    def _(s):
        mag_t[s] = mag[s].T

    def step(t, op, next_summed, last):
        next_op = jnp.add if next_summed else jnp.maximum
        row.group_to_back(t, op)
        row.finish_back(t)
        if not last:
            col_pass(t + 1, next_summed)
        col.group_to_back(t, op)
        if not last:
            col.pair_to_group(t + 1, next_op)
        col.finish_back(t)
        if not last:
            row_pass(t + 1, next_summed)
            row.pair_to_group(t + 1, next_op)

    @pl.loop(0, SWEEPS - 1)
    def _(t):
        step(t, jnp.maximum, False, False)

    step(SWEEPS - 1, jnp.maximum, True, False)
    step(SWEEPS, jnp.add, False, True)
    r_out[...] = r_fac[ROUNDS]
    c_out[...] = c_fac[ROUNDS]


def final_kernel(rows, cols, count, tiles, r_fac, c_fac, out, held, made, zero, in_sem, out_sem):
    slots, size = tiles.shape[0], tiles.shape[1]
    group = GROUP if slots % GROUP == 0 else 1
    lanes = 128
    live = count[0]

    def load(s):
        return pltpu.make_async_copy(tiles.at[s], held.at[s], in_sem.at[s])

    def store(s):
        return pltpu.make_async_copy(made.at[s], out.at[s], out_sem.at[s])

    @pl.loop(0, slots)
    def _(s):
        @pl.when(s // group * group < live)
        def _():
            load(s).start()

    zero[...] = jnp.zeros_like(zero)

    @pl.loop(0, slots // group)
    def _(g):
        base = g * group

        @pl.when(base >= live)
        def _():
            for k in range(group):
                pltpu.make_async_copy(zero, out.at[base + k], out_sem.at[base + k]).start()

    @pl.loop(0, slots // group)
    def _(g):
        base = g * group

        @pl.when(base < live)
        def _():
            for k in range(group):
                load(base + k).wait()
            for k in range(group):
                s = base + k
                r = jnp.where(s < live, r_fac[pl.ds(rows[s], 1), :], jnp.float32(0.0))
                c = c_fac[pl.ds(cols[s], 1), :]
                rt = jnp.broadcast_to(r, (lanes, size)).T
                for j in range(0, size, lanes):
                    made[s, :, j:j + lanes] = held[s, :, j:j + lanes] * rt * c[:, j:j + lanes]
            for k in range(group):
                store(base + k).start()

    @pl.loop(0, slots)
    def _(s):
        store(s).wait()


def shards(tiles, tile_rows, tile_cols, tile_count):
    values = tiles[0, 0]
    rows = tile_rows.reshape(-1)
    cols = tile_cols.reshape(-1)
    count = tile_count.reshape(-1)
    slots, size = values.shape[0], values.shape[1]
    n_row, n_col, depths = lax.axis_size("row"), lax.axis_size("col"), lax.axis_size("depth")
    col_blocks = n_row * depths * ANCHORS
    rh, ch = RB_DEV // depths, col_blocks // depths
    f32 = jnp.float32
    dma = pltpu.SemaphoreType.DMA
    d1 = depths - 1
    smem = pl.BlockSpec(memory_space=pltpu.SMEM)
    vmem = pl.BlockSpec(memory_space=pltpu.VMEM)
    row_scale, col_scale = pl.pallas_call(
        scale_kernel,
        out_shape=(
            jax.ShapeDtypeStruct((depths, rh, size), f32),
            jax.ShapeDtypeStruct((depths, ch, size), f32),
        ),
        in_specs=[smem, smem, smem, pl.BlockSpec(memory_space=pl.ANY)],
        out_specs=(vmem, vmem),
        scratch_shapes=[
            pltpu.VMEM((slots, size, size), f32),
            pltpu.VMEM((slots, size, size), f32),
            dma((slots,)),
            pltpu.VMEM((ROUNDS + 1, depths, rh, size), f32),
            pltpu.VMEM((ROUNDS + 1, depths, ch, size), f32),
            pltpu.VMEM((slots, 1, size), f32),
            pltpu.VMEM((slots, 1, size), f32),
            pltpu.VMEM((ROUNDS, depths, rh, size), f32),
            pltpu.VMEM((ROUNDS, depths, ch, size), f32),
            pltpu.VMEM((ROUNDS, d1, rh, size), f32),
            pltpu.VMEM((ROUNDS, d1, ch, size), f32),
            pltpu.VMEM((ROUNDS, rh, size), f32),
            pltpu.VMEM((ROUNDS, ch, size), f32),
            pltpu.VMEM((ROUNDS, n_col - 1, rh, size), f32),
            pltpu.VMEM((ROUNDS, n_row - 1, ch, size), f32),
            dma((ROUNDS, d1)), dma((ROUNDS, d1)), dma((ROUNDS, d1)), dma((ROUNDS, d1)),
            dma((ROUNDS, d1)), dma((ROUNDS, d1)), dma((ROUNDS, d1)), dma((ROUNDS, d1)),
            dma((ROUNDS, n_col - 1)), dma((ROUNDS, n_col - 1)),
            dma((ROUNDS, n_row - 1)), dma((ROUNDS, n_row - 1)),
        ],
        compiler_params=pltpu.CompilerParams(
            collective_id=0, has_side_effects=True, vmem_limit_bytes=60 * 2**20
        ),
        name="equilibrate",
    )(rows, cols, count, values)
    row_scale = row_scale.reshape(depths * rh, size)
    col_scale = col_scale.reshape(depths * ch, size)

    scaled = pl.pallas_call(
        final_kernel,
        in_specs=[smem, smem, smem, pl.BlockSpec(memory_space=pl.ANY), vmem, vmem],
        out_specs=pl.BlockSpec(memory_space=pl.ANY),
        out_shape=jax.ShapeDtypeStruct(values.shape, f32),
        scratch_shapes=[
            pltpu.VMEM(values.shape, f32),
            pltpu.VMEM(values.shape, f32),
            pltpu.VMEM((size, size), f32),
            dma((slots,)),
            dma((slots,)),
        ],
        compiler_params=pltpu.CompilerParams(vmem_limit_bytes=60 * 2**20),
        name="scale_tiles",
    )(rows, cols, count, values, row_scale, col_scale)
    return (row_scale.reshape(-1), col_scale.reshape(-1), scaled[None, None])


def solution(mesh):
    in_specs = (
        P("row", "col", "depth", None, None),
        P("row", "col", "depth"),
        P("row", "col", "depth"),
        P("row", "col", "depth"),
    )
    out_specs = (P("row"), P("col"), P("row", "col", "depth", None, None))
    return jax.shard_map(shards, mesh=mesh, in_specs=in_specs, out_specs=out_specs, check_vma=False)
```
